512 devices in a mesh: dp: 32 (over z_hi, y, core), seq: 16 (over z_lo, x).
Axes of the slice: x: 4, y: 8, z: 8 (z_hi: 2, z_lo: 4; z = z_hi * 4 + z_lo), core: 2. Of those that a mesh axis runs over, the one named last changes fastest.
Arguments:
- img_qkv: bfloat16 [32, 1792, 3, 2048], P('dp', 'seq'), may hold values from -6 to 6
- txt_qkv: bfloat16 [32, 256, 3, 2048], P('dp', 'seq'), may hold values from -6 to 6
- img_cot: bfloat16 [32, 1792, 2048], P('dp', 'seq'), may hold values from -48 to 48
- txt_cot: bfloat16 [32, 256, 2048], P('dp', 'seq'), may hold values from -48 to 48
- norm_gains: float32 [4, 128], replicated, may hold values from 0.5 to 2
Outputs:
- img_out: bfloat16 [32, 1792, 2048], P('dp', 'seq')
- txt_out: bfloat16 [32, 256, 2048], P('dp', 'seq')
- img_grad: bfloat16 [32, 1792, 3, 2048], P('dp', 'seq')
- txt_grad: bfloat16 [32, 256, 3, 2048], P('dp', 'seq')
- gain_grad: float32 [512], P('dp')
The draws below stay inside these ranges and needn't reach their ends.
All inputs are finite; a program needn't handle non-finite values.
Results may differ from the reference program's by a relative error of at most 0.012.
The reference program's roundings to bfloat16 on the way count: a program that leaves them out, or rounds other values in their place, can miss the bound.
Values may be sent and summed in bfloat16 or wider, within the bound.
A program may use at most 128 MiB of HBM per device.

```python
import math
import jax
import jax.numpy as jnp
from jax import lax

HD = 128
HEADS = 16
HW = 2048
GRID_W = 64
IMG = 1792
TXT = 256
SAMPLES = 32


def levels(rng, shape, split, low, top_value):
    gain = 1.0
    for dim, parts in split:
        draws = jax.random.uniform(jax.random.fold_in(jax.random.fold_in(rng, 6), dim), (parts,), jnp.float32, low / len(split), top_value / len(split))
        gain = gain * jnp.repeat(jnp.exp(draws), shape[dim] // parts).reshape((-1,) + (1,) * (len(shape) - 1 - dim))
    return gain


def normal_values(stream_key, shape, width, most, split=(), kind=jnp.bfloat16):
    level = levels(stream_key, shape, split, -0.22, 0.18) if split else 1.0
    drawn = jax.random.normal(stream_key, shape, jnp.float32) * width * level
    return jnp.minimum(jnp.maximum(drawn, -most), most).astype(kind)


def setup_inputs(seed: int = 0) -> dict:
    seeds = jax.random.split(jax.random.key(seed), 6)
    return {
        "img_qkv": normal_values(seeds[0], (SAMPLES, IMG, 3, HW), 1.0, 6.0, ((0, 32), (1, 16))),
        "txt_qkv": normal_values(seeds[1], (SAMPLES, TXT, 3, HW), 1.0, 6.0, ((0, 32), (1, 16))),
        "img_cot": normal_values(seeds[2], (SAMPLES, IMG, HW), 8.0, 48.0, ((0, 32), (1, 16))),
        "txt_cot": normal_values(seeds[3], (SAMPLES, TXT, HW), 8.0, 48.0, ((0, 32), (1, 16))),
        "norm_gains": jnp.clip(jnp.exp(jax.random.uniform(seeds[4], (4, HD), jnp.float32, math.log(0.5), math.log(2.0))), 0.5, 2.0),
    }


EPSILON = 1e-06

def rope_tables(seq_len, text_len, grid_w, head_dim):
    position = jnp.arange(seq_len, dtype=jnp.int32)
    image_pos = jnp.maximum(position - text_len, 0)
    image_col = (position >= text_len).astype(jnp.float32)
    row_pos = (image_pos // grid_w).astype(jnp.float32) * image_col
    col_pos = (image_pos % grid_w).astype(jnp.float32) * image_col
    time_dims = head_dim // 8
    axis_dims = (head_dim - time_dims) // 2
    channel = jnp.arange(head_dim, dtype=jnp.int32)
    in_rows = (channel >= time_dims) & (channel < time_dims + axis_dims)
    in_cols = channel >= time_dims + axis_dims
    within = jnp.where(in_cols, channel - time_dims - axis_dims, channel - time_dims)
    within = jnp.maximum(within, 0) // 2
    frequency = jnp.power(jnp.float32(10000.0), -2.0 * within.astype(jnp.float32) / axis_dims)
    angles = jnp.where(in_rows[None, :], row_pos[:, None] * frequency[None, :], jnp.float32(0.0))
    angles = jnp.where(in_cols[None, :], col_pos[:, None] * frequency[None, :], angles)
    row_idx = channel[:, None]
    col_idx = channel[None, :]
    plus_one = ((row_idx % 2 == 0) & (col_idx == row_idx + 1)).astype(jnp.float32)
    minus_one = ((row_idx % 2 == 1) & (col_idx == row_idx - 1)).astype(jnp.float32)
    swap_mat = plus_one - minus_one
    return (jnp.cos(angles), jnp.sin(angles), swap_mat, image_col[:, None])

def rms_rows(values_in):
    inverse = lax.rsqrt(lax.optimization_barrier(jnp.mean(values_in * values_in, axis=-1, keepdims=True)) + EPSILON)
    return (values_in * inverse, inverse)

def rms_back(grad_hat, hat_vals, inverse):
    middle = lax.optimization_barrier(jnp.mean(grad_hat * hat_vals, axis=-1, keepdims=True))
    return (grad_hat - hat_vals * middle) * inverse

def rotate(values_in, tables):
    cos_t, sin_t, swap_mat, image_col = tables
    turned = jnp.dot(values_in, swap_mat, precision=lax.Precision.HIGHEST)
    return values_in * cos_t + turned * sin_t

def unrotate(grad_in, tables):
    cos_t, sin_t, swap_mat, image_col = tables
    turned = jnp.dot(grad_in * sin_t, swap_mat.T, precision=lax.Precision.HIGHEST)
    return grad_in * cos_t + turned

def head_pass(q_raw, k_raw, value, d_out, norm_gains, tables):
    image_col = tables[3]
    head_dim = q_raw.shape[1]
    attn_scale = 1.0 / math.sqrt(head_dim)
    q_hat, q_inv = rms_rows(q_raw)
    k_hat, k_inv = rms_rows(k_raw)
    q_gain = jnp.where(image_col > 0.5, norm_gains[0][None, :], norm_gains[2][None, :])
    k_gain = jnp.where(image_col > 0.5, norm_gains[1][None, :], norm_gains[3][None, :])
    q_rot = rotate(q_hat * q_gain, tables).astype(jnp.bfloat16)
    k_rot = rotate(k_hat * k_gain, tables).astype(jnp.bfloat16)
    scores = jnp.dot(q_rot, k_rot.T, preferred_element_type=jnp.float32) * attn_scale
    exp_scores = jnp.exp(scores)
    prob_full = exp_scores / lax.optimization_barrier(jnp.sum(exp_scores, axis=1, keepdims=True))
    prob_half = prob_full.astype(jnp.bfloat16)
    attn_out = jnp.dot(prob_half, value, preferred_element_type=jnp.float32).astype(jnp.bfloat16)
    row_delta = lax.optimization_barrier(jnp.sum(d_out.astype(jnp.float32) * attn_out.astype(jnp.float32), axis=1, keepdims=True))
    d_value = jnp.dot(prob_half.T, d_out, preferred_element_type=jnp.float32)
    d_prob = jnp.dot(d_out, value.T, preferred_element_type=jnp.float32)
    d_score = (prob_full * (d_prob - row_delta) * attn_scale).astype(jnp.bfloat16)
    dq_rot = jnp.dot(d_score, k_rot, preferred_element_type=jnp.float32)
    dk_rot = jnp.dot(d_score.T, q_rot, preferred_element_type=jnp.float32)
    dq_norm = unrotate(dq_rot, tables)
    dk_norm = unrotate(dk_rot, tables)
    text_col = 1.0 - image_col
    gain_terms = jnp.stack([lax.optimization_barrier(jnp.sum(dq_norm * q_hat * image_col, axis=0)), lax.optimization_barrier(jnp.sum(dk_norm * k_hat * image_col, axis=0)), lax.optimization_barrier(jnp.sum(dq_norm * q_hat * text_col, axis=0)), lax.optimization_barrier(jnp.sum(dk_norm * k_hat * text_col, axis=0))])
    d_query = rms_back(dq_norm * q_gain, q_hat, q_inv)
    d_key = rms_back(dk_norm * k_gain, k_hat, k_inv)
    return (attn_out, d_query.astype(jnp.bfloat16), d_key.astype(jnp.bfloat16), d_value.astype(jnp.bfloat16), gain_terms)

def reference(img_qkv, txt_qkv, img_cot, txt_cot, norm_gains):
    seq_len = TXT + IMG
    tables = rope_tables(seq_len, TXT, GRID_W, HD)
    joint = jnp.concatenate([txt_qkv, img_qkv], axis=1).reshape(SAMPLES, seq_len, 3, HEADS, HD)
    joint = jnp.transpose(joint, (0, 3, 1, 2, 4)).reshape(SAMPLES * HEADS, seq_len, 3, HD)
    joint_cot = jnp.concatenate([txt_cot, img_cot], axis=1).reshape(SAMPLES, seq_len, HEADS, HD)
    joint_cot = jnp.transpose(joint_cot, (0, 2, 1, 3)).reshape(SAMPLES * HEADS, seq_len, HD)

    def one_head(pieces):
        projected, grad_out = pieces
        return head_pass(projected[:, 0].astype(jnp.float32), projected[:, 1].astype(jnp.float32), projected[:, 2], grad_out, norm_gains, tables)
    attn_out, d_query, d_key, d_value, gain_terms = lax.map(one_head, (joint, joint_cot))
    attn_out = jnp.transpose(attn_out.reshape(SAMPLES, HEADS, seq_len, HD), (0, 2, 1, 3)).reshape(SAMPLES, seq_len, HEADS * HD)
    grads = jnp.stack([d_query, d_key, d_value], axis=2).reshape(SAMPLES, HEADS, seq_len, 3, HD)
    grads = jnp.transpose(grads, (0, 2, 3, 1, 4)).reshape(SAMPLES, seq_len, 3, HEADS * HD)
    grad_scale = 1.0 / math.sqrt(SAMPLES * seq_len * HEADS)
    gain_grad = (lax.optimization_barrier(jnp.sum(gain_terms, axis=0)) * grad_scale).reshape(4 * HD)
    return (attn_out[:, TXT:], attn_out[:, :TXT], grads[:, TXT:], grads[:, :TXT], gain_grad)
```

```python
import functools
import math

import jax
import jax.numpy as jnp
import numpy as np
from jax import lax
from jax.experimental import pallas as pl
from jax.experimental.pallas import tpu as pltpu
from jax.sharding import PartitionSpec as P

HD = 128
GRID_W = 64
EPSILON = 1e-06
F32 = jnp.float32
BF16 = jnp.bfloat16
SCALE = 1.0 / math.sqrt(HD)
LOG2E_SCALE = SCALE * math.log2(math.e)
NT = (((1,), (1,)), ((), ()))
BLK = 128
TXT_B = 16
QB = 256
GRAD_SCALE = 1.0 / math.sqrt(32 * 2048 * 16)
KC = 512


def small_tables(n_rows):
    time_dims = HD // 8
    axis = (HD - time_dims) // 2
    channel = np.arange(HD)
    in_rows = (channel >= time_dims) & (channel < time_dims + axis)
    in_cols = channel >= time_dims + axis
    within = np.where(in_cols, channel - time_dims - axis, channel - time_dims)
    within = np.maximum(within, 0) // 2
    freq = np.power(10000.0, -2.0 * within / axis).astype(np.float32)
    sign = np.where(channel % 2 == 0, -1.0, 1.0)
    rows = np.arange(n_rows, dtype=np.float32)[:, None] * np.where(in_rows, freq, 0)[None, :]
    cols = np.arange(GRID_W, dtype=np.float32)[:, None] * np.where(in_cols, freq, 0)[None, :]
    rows, cols = rows.astype(np.float32).astype(np.float64), cols.astype(np.float32).astype(np.float64)
    out = [np.cos(rows), np.sin(rows) * sign, np.cos(cols), np.sin(cols) * sign]
    return [o.astype(np.float32) for o in out]


def fill_tables(rc, rs, cc, cs, cos_ref, sin_ref):
    lane = lax.broadcasted_iota(jnp.int32, (16, HD), 1)
    is_col = lane >= HD // 8 + (HD - HD // 8) // 2

    def text(b, c):
        cos_ref[b, pl.ds(0, TXT_B), :] = jnp.ones((TXT_B, HD), F32)
        sin_ref[b, pl.ds(0, TXT_B), :] = jnp.zeros((TXT_B, HD), F32)
        return c

    lax.fori_loop(0, 16, text, 0)

    def image(m, c):
        b, off = m // 7, pl.multiple_of(16 + 16 * (m % 7), 16)
        r, col = m // 4, pl.multiple_of(16 * (m % 4), 16)
        cos_ref[b, pl.ds(off, 16), :] = jnp.where(is_col, cc[pl.ds(col, 16), :], rc[pl.ds(r, 1), :])
        sin_ref[b, pl.ds(off, 16), :] = jnp.where(is_col, cs[pl.ds(col, 16), :], rs[pl.ds(r, 1), :])
        return c

    lax.fori_loop(0, 112, image, 0)


def swap_pairs(x):
    lane = lax.broadcasted_iota(jnp.int32, x.shape, x.ndim - 1)
    return jnp.where(lane % 2 == 0, pltpu.roll(x, HD - 1, axis=1), pltpu.roll(x, 1, axis=1))


def normed(x):
    inv = lax.rsqrt(jnp.mean(x * x, axis=-1, keepdims=True) + EPSILON)
    return x * inv, inv


def gain_rows(gains, which):
    row = lax.broadcasted_iota(jnp.int32, (BLK, HD), 0)
    img = jnp.broadcast_to(gains[which : which + 1, :], (BLK, HD))
    txt = jnp.broadcast_to(gains[which + 2 : which + 3, :], (BLK, HD))
    return jnp.where(row < TXT_B, txt, img)


def rope_block(raw, gain, cos, sin):
    hat, _ = normed(raw.astype(F32))
    x = hat * gain
    return (x * cos + swap_pairs(x) * sin).astype(BF16)


def back_block(raw, d_rot, gain, cos, sin):
    hat, inv = normed(raw.astype(F32))
    d_norm = d_rot * cos + swap_pairs(d_rot * sin)
    terms = d_norm * hat
    scaled = d_norm * gain
    middle = jnp.mean(scaled * hat, axis=-1, keepdims=True)
    return ((scaled - hat * middle) * inv).astype(BF16), terms[:TXT_B], terms[TXT_B:]


def fold8(x):
    total = x[0:8]
    for i in range(8, x.shape[0], 8):
        total = total + x[i : i + 8]
    return total


def prep_k(b, kin, vin, gains, cos_ref, sin_ref, kr, krt, vt):
    k = rope_block(kin[b], gain_rows(gains, 1), cos_ref[b], sin_ref[b])
    kr[b] = k
    krt[b] = k.T
    vt[b] = vin[b].T


def prep_q(b, qin, gains, cos_ref, sin_ref, qr):
    qr[b] = rope_block(qin[b], gain_rows(gains, 0), cos_ref[b], sin_ref[b])


def cat_t(ref, c, n):
    return jnp.concatenate([ref[c * n + i] for i in range(n)], axis=1)


def forward(i, kr, vt, qr, eb, oout, inv_l):
    n = KC // BLK
    two = pl.ds(2 * i, 2)
    q = qr[two].reshape(QB, HD)
    total = jnp.zeros((8, QB), F32)
    acc = jnp.zeros((HD, QB), F32)
    for c in range(16 // n):
        keys = kr[c * n : (c + 1) * n].reshape(KC, HD)
        s = lax.dot_general(keys, q, NT, preferred_element_type=F32)
        e = jnp.exp2(s * LOG2E_SCALE)
        total = total + fold8(e)
        e16 = e.astype(BF16)
        eb[i, pl.ds(c * KC, KC), :] = e16
        acc = acc + jnp.dot(cat_t(vt, c, n), e16, preferred_element_type=F32)
    inv = 1.0 / jnp.sum(total, axis=0, keepdims=True)
    inv_l[i] = jnp.broadcast_to(inv, (8, QB))
    oout[two] = (acc * inv).T.astype(BF16).reshape(2, BLK, HD)


def backward(i, first, gin, vin, kr, krt, qr, oout, eb, inv_l, dkacc, dvacc, dqrot):
    n = KC // BLK
    two = pl.ds(2 * i, 2)
    g = gin[two].reshape(QB, HD).astype(F32)
    o = oout[two].reshape(QB, HD).astype(F32)
    inv = inv_l[i][0:1, :]
    delta = jnp.sum((g * o).T, axis=0, keepdims=True) * inv
    gt = (g.T * inv).astype(BF16)
    gs = gt.T
    q = qr[two].reshape(QB, HD)
    acc = jnp.zeros((HD, QB), F32)
    for c in range(16 // n):
        rows = pl.ds(c * KC, KC)
        e16 = eb[i, rows, :]
        values = vin[c * n : (c + 1) * n].reshape(KC, HD)
        dp = jnp.dot(values, gt, preferred_element_type=F32)
        ds = (e16.astype(F32) * (dp - delta)).astype(BF16)
        dv = jnp.dot(e16, gs, preferred_element_type=F32)
        dk = jnp.dot(ds, q, preferred_element_type=F32)
        if first:
            dvacc[rows, :] = dv
            dkacc[rows, :] = dk
        else:
            dvacc[rows, :] += dv
            dkacc[rows, :] += dk
        acc = acc + jnp.dot(cat_t(krt, c, n), ds, preferred_element_type=F32)
    dqrot[...] = (acc * SCALE).T.reshape(2, BLK, HD)


def finish(b, raw, d_rot, which, gains, cos_ref, sin_ref, out, gsum):
    d, txt, img = back_block(raw[b], d_rot, gain_rows(gains, which), cos_ref[b], sin_ref[b])
    out[b] = d
    gsum[which] += fold8(img)
    gsum[which + 2] += fold8(txt)


def attention_kernel(qin, kin, vin, gin, gains, rc, rs, cc, cs, oout, dq, dk, dv, gout,
                     cos_ref, sin_ref, kr, krt, vt, qr, eb, inv_l, dkacc, dvacc, dqrot, gsum):
    fill_tables(rc, rs, cc, cs, cos_ref, sin_ref)
    gsum[...] = jnp.zeros_like(gsum)
    g = gains[...]

    def prep(b, c):
        prep_k(b, kin, vin, g, cos_ref, sin_ref, kr, krt, vt)
        prep_q(b, qin, g, cos_ref, sin_ref, qr)
        return c

    lax.fori_loop(0, 16, prep, 0)
    dkacc[...] = jnp.zeros_like(dkacc)
    dvacc[...] = jnp.zeros_like(dvacc)

    def step(i, c):
        forward(i, kr, vt, qr, eb, oout, inv_l)
        return c

    lax.fori_loop(0, 8, step, 0)

    def step2(i, c):
        backward(i, False, gin, vin, kr, krt, qr, oout, eb, inv_l, dkacc, dvacc, dqrot)
        for j in range(2):
            finish(2 * i + j, qin, dqrot[j], 0, g, cos_ref, sin_ref, dq, gsum)
        return c

    lax.fori_loop(0, 8, step2, 0)

    def last(b, c):
        rows = pl.ds(pl.multiple_of(b * BLK, BLK), BLK)
        finish(b, kin, dkacc[rows, :] * SCALE, 1, g, cos_ref, sin_ref, dk, gsum)
        dv[b] = dvacc[rows, :].astype(BF16)
        return c

    lax.fori_loop(0, 16, last, 0)
    for j in range(4):
        gout[j : j + 1, :] = jnp.sum(gsum[j], axis=0, keepdims=True)


def compute_scratch():
    return [
        pltpu.VMEM((16, BLK, HD), F32), pltpu.VMEM((16, BLK, HD), F32),
        pltpu.VMEM((16, BLK, HD), BF16), pltpu.VMEM((16, HD, BLK), BF16), pltpu.VMEM((16, HD, BLK), BF16),
        pltpu.VMEM((16, BLK, HD), BF16),
        pltpu.VMEM((8, 2048, QB), BF16), pltpu.VMEM((8, 8, QB), F32),
        pltpu.VMEM((2048, HD), F32), pltpu.VMEM((2048, HD), F32),
        pltpu.VMEM((2, BLK, HD), F32), pltpu.VMEM((4, 8, HD), F32),
    ]


def attention(q, k, v, g, gains):
    block = jax.ShapeDtypeStruct((16, BLK, HD), BF16)
    V = pl.BlockSpec(memory_space=pltpu.VMEM)
    return pl.pallas_call(
        attention_kernel,
        out_shape=[block] * 4 + [jax.ShapeDtypeStruct((4, HD), F32)],
        in_specs=[V] * 9, out_specs=[V] * 5,
        scratch_shapes=compute_scratch(),
        compiler_params=pltpu.CompilerParams(vmem_limit_bytes=56 << 20),
    )(q, k, v, g, gains, *[jnp.asarray(t) for t in small_tables(28)])


def spread(n, axis, fn):
    me = lax.axis_index(axis)

    def one(r, c):
        fn(lax.rem(me + r, n))
        return c

    lax.fori_loop(1, n, one, 0)


def barrier(axes):
    sem = pltpu.get_barrier_semaphore()
    for axis, n in axes:
        spread(n, axis, lambda d, axis=axis: pl.semaphore_signal(
            sem, inc=1, device_id={axis: d}, device_id_type=pl.DeviceIdType.MESH))
    pl.semaphore_wait(sem, sum(n - 1 for _, n in axes))


def remote(src, dst, send, recv, axis, d):
    return pltpu.make_async_remote_copy(src, dst, send, recv, device_id={axis: d}, device_id_type=pl.DeviceIdType.MESH)


def wait_bytes(ref, sem):
    pltpu.make_async_copy(ref, ref, sem).wait()


def head_columns(d):
    return pl.ds(pl.multiple_of(d * HD, HD), HD)


def gather_kernel(img, txt, img_cot, txt_cot, qin, kin, vin, gin, send, recv, local):
    me = lax.axis_index("seq")
    barrier((("seq", 16),))
    text, image = pl.ds(0, TXT_B), pl.ds(TXT_B, BLK - TXT_B)

    def pieces(slot, d):
        col = head_columns(d)
        if slot < 3:
            return txt.at[slot, :, col], img.at[slot, :, col]
        return txt_cot.at[:, col], img_cot.at[:, col]

    slots = ((1, kin), (0, qin), (2, vin), (3, gin))
    for slot, ref in slots:
        def push(d, slot=slot, ref=ref):
            t, i = pieces(slot, d)
            remote(t, ref.at[me, text], send.at[slot], recv.at[slot], "seq", d).start()
            remote(i, ref.at[me, image], send.at[slot], recv.at[slot], "seq", d).start()

        spread(16, "seq", push)
        t, i = pieces(slot, me)
        pltpu.make_async_copy(t, ref.at[me, text], local.at[slot]).start()
        pltpu.make_async_copy(i, ref.at[me, image], local.at[slot]).start()
    for slot, ref in slots:
        wait_bytes(ref.at[0], local.at[slot])
        wait_bytes(ref.at[pl.ds(0, 15)], recv.at[slot])
        wait_bytes(ref.at[pl.ds(0, 15)], send.at[slot])


def scatter_kernel(o, dq, dk, dv, part, img_out, txt_out, img_grad, txt_grad, gain,
                   rows, srow, srows, send, recv, local, gsend, grecv):
    me, dp = lax.axis_index("seq"), lax.axis_index("dp")
    barrier((("seq", 16), ("dp", 32)))
    spread(32, "dp", lambda d: remote(part.at[d // 8], rows.at[dp], gsend.at[0], grecv.at[0], "dp", d).start())
    text, image = pl.ds(0, TXT_B), pl.ds(TXT_B, BLK - TXT_B)
    col = head_columns(me)
    slots = ((0, dq), (1, dk), (2, dv), (3, o))

    def target(slot):
        if slot < 3:
            return txt_grad.at[slot, :, col], img_grad.at[slot, :, col]
        return txt_out.at[:, col], img_out.at[:, col]

    for slot, ref in slots:
        t, i = target(slot)

        def push(d, slot=slot, ref=ref, t=t, i=i):
            remote(ref.at[d, text], t, send.at[slot], recv.at[slot], "seq", d).start()
            remote(ref.at[d, image], i, send.at[slot], recv.at[slot], "seq", d).start()

        spread(16, "seq", push)
        pltpu.make_async_copy(ref.at[me, text], t, local.at[slot]).start()
        pltpu.make_async_copy(ref.at[me, image], i, local.at[slot]).start()
    rows[dp] = part[dp // 8]
    wait_bytes(rows.at[pl.ds(0, 31)], grecv.at[0])
    srow[...] = jnp.sum(rows[...], axis=0)
    spread(16, "seq", lambda d: remote(srow, srows.at[me], gsend.at[1], grecv.at[1], "seq", d).start())
    srows[me] = srow[...]
    wait_bytes(srows.at[pl.ds(0, 15)], grecv.at[1])
    total = jnp.sum(srows[...], axis=0) * GRAD_SCALE
    gain[...] = pltpu.roll(jnp.broadcast_to(total, (8, HD)), lax.rem(HD - lax.rem(dp, 8) * 16, HD), axis=1)
    wait_bytes(rows.at[pl.ds(0, 31)], gsend.at[0])
    wait_bytes(srows.at[pl.ds(0, 15)], gsend.at[1])
    for slot, ref in slots:
        wait_bytes(ref.at[0], local.at[slot])
        wait_bytes(ref.at[pl.ds(0, 15)], send.at[slot])
        wait_bytes(ref.at[pl.ds(0, 15)], recv.at[slot])


def per_device(img_qkv, txt_qkv, img_cot, txt_cot, norm_gains):
    img = jnp.transpose(img_qkv[0], (1, 0, 2))
    txt = jnp.transpose(txt_qkv[0], (1, 0, 2))
    any_, vmem = pl.BlockSpec(memory_space=pl.ANY), pl.BlockSpec(memory_space=pltpu.VMEM)
    block = jax.ShapeDtypeStruct((16, BLK, HD), BF16)
    dma = pltpu.SemaphoreType.DMA
    q, k, v, g = pl.pallas_call(
        gather_kernel, out_shape=[block] * 4, in_specs=[any_] * 4, out_specs=[vmem] * 4,
        scratch_shapes=[dma((4,))] * 3,
        compiler_params=pltpu.CompilerParams(collective_id=0, has_side_effects=True, vmem_limit_bytes=16 << 20),
    )(img, txt, img_cot[0], txt_cot[0])
    o, dq, dk, dv, part = attention(q, k, v, g, norm_gains)
    shape = lambda s: jax.ShapeDtypeStruct(s, BF16)
    n_img, n_txt, width = img.shape[1], txt.shape[1], img.shape[2]
    img_out, txt_out, img_grad, txt_grad, gain = pl.pallas_call(
        scatter_kernel,
        out_shape=[shape((n_img, width)), shape((n_txt, width)), shape((3, n_img, width)), shape((3, n_txt, width)),
                   jax.ShapeDtypeStruct((8, HD), F32)],
        in_specs=[vmem] * 5, out_specs=[any_] * 4 + [vmem],
        scratch_shapes=[pltpu.VMEM((32, 1, HD), F32), pltpu.VMEM((1, HD), F32), pltpu.VMEM((16, 1, HD), F32),
                        dma((4,)), dma((4,)), dma((4,)), dma((2,)), dma((2,))],
        compiler_params=pltpu.CompilerParams(collective_id=1, has_side_effects=True, vmem_limit_bytes=16 << 20),
    )(o, dq, dk, dv, part.reshape(4, 1, HD))
    return (img_out[None], txt_out[None], jnp.transpose(img_grad, (1, 0, 2))[None],
            jnp.transpose(txt_grad, (1, 0, 2))[None], gain[0, :16])


def solution(mesh):
    in_specs = (P("dp", "seq", None, None), P("dp", "seq", None, None), P("dp", "seq", None), P("dp", "seq", None), P())
    out_specs = (P("dp", "seq", None), P("dp", "seq", None), P("dp", "seq", None, None), P("dp", "seq", None, None), P("dp"))
    return jax.shard_map(per_device, mesh=mesh, in_specs=in_specs, out_specs=out_specs, check_vma=False)
```

```python
import functools
import math

import jax
import jax.numpy as jnp
import numpy as np
from jax import lax
from jax.experimental import pallas as pl
from jax.experimental.pallas import tpu as pltpu
from jax.sharding import PartitionSpec as P

HD = 128
GRID_W = 64
EPSILON = 1e-06
F32 = jnp.float32
BF16 = jnp.bfloat16
SCALE = 1.0 / math.sqrt(HD)
LOG2E_SCALE = SCALE * math.log2(math.e)
NT = (((1,), (1,)), ((), ()))
BLK = 128
TXT_B = 16
QB = 256
GRAD_SCALE = 1.0 / math.sqrt(32 * 2048 * 16)
KC = 512


def small_tables(n_rows):
    time_dims = HD // 8
    axis = (HD - time_dims) // 2
    channel = np.arange(HD)
    in_rows = (channel >= time_dims) & (channel < time_dims + axis)
    in_cols = channel >= time_dims + axis
    within = np.where(in_cols, channel - time_dims - axis, channel - time_dims)
    within = np.maximum(within, 0) // 2
    freq = np.power(10000.0, -2.0 * within / axis).astype(np.float32)
    sign = np.where(channel % 2 == 0, -1.0, 1.0)
    rows = np.arange(n_rows, dtype=np.float32)[:, None] * np.where(in_rows, freq, 0)[None, :]
    cols = np.arange(GRID_W, dtype=np.float32)[:, None] * np.where(in_cols, freq, 0)[None, :]
    rows, cols = rows.astype(np.float32).astype(np.float64), cols.astype(np.float32).astype(np.float64)
    out = [np.cos(rows), np.sin(rows) * sign, np.cos(cols), np.sin(cols) * sign]
    return [o.astype(np.float32) for o in out]


def fill_tables(rc, rs, cc, cs, cos_ref, sin_ref):
    lane = lax.broadcasted_iota(jnp.int32, (16, HD), 1)
    is_col = lane >= HD // 8 + (HD - HD // 8) // 2

    def text(b, c):
        cos_ref[b, pl.ds(0, TXT_B), :] = jnp.ones((TXT_B, HD), F32)
        sin_ref[b, pl.ds(0, TXT_B), :] = jnp.zeros((TXT_B, HD), F32)
        return c

    lax.fori_loop(0, 16, text, 0)

    def image(m, c):
        b, off = m // 7, pl.multiple_of(16 + 16 * (m % 7), 16)
        r, col = m // 4, pl.multiple_of(16 * (m % 4), 16)
        cos_ref[b, pl.ds(off, 16), :] = jnp.where(is_col, cc[pl.ds(col, 16), :], rc[pl.ds(r, 1), :])
        sin_ref[b, pl.ds(off, 16), :] = jnp.where(is_col, cs[pl.ds(col, 16), :], rs[pl.ds(r, 1), :])
        return c

    lax.fori_loop(0, 112, image, 0)


def swap_pairs(x):
    lane = lax.broadcasted_iota(jnp.int32, x.shape, x.ndim - 1)
    return jnp.where(lane % 2 == 0, pltpu.roll(x, HD - 1, axis=1), pltpu.roll(x, 1, axis=1))


def normed(x):
    inv = lax.rsqrt(jnp.mean(x * x, axis=-1, keepdims=True) + EPSILON)
    return x * inv, inv


def gain_rows(gains, which):
    row = lax.broadcasted_iota(jnp.int32, (BLK, HD), 0)
    img = jnp.broadcast_to(gains[which : which + 1, :], (BLK, HD))
    txt = jnp.broadcast_to(gains[which + 2 : which + 3, :], (BLK, HD))
    return jnp.where(row < TXT_B, txt, img)


def rope_block(raw, gain, cos, sin):
    hat, _ = normed(raw.astype(F32))
    x = hat * gain
    return (x * cos + swap_pairs(x) * sin).astype(BF16)


def back_block(raw, d_rot, gain, cos, sin):
    hat, inv = normed(raw.astype(F32))
    d_norm = d_rot * cos + swap_pairs(d_rot * sin)
    terms = d_norm * hat
    scaled = d_norm * gain
    middle = jnp.mean(scaled * hat, axis=-1, keepdims=True)
    return ((scaled - hat * middle) * inv).astype(BF16), terms[:TXT_B], terms[TXT_B:]


def fold8(x):
    total = x[0:8]
    for i in range(8, x.shape[0], 8):
        total = total + x[i : i + 8]
    return total


def cat_t(ref, c, n):
    return jnp.concatenate([ref[c * n + i] for i in range(n)], axis=1)


def forward(i, kr, vt, qr, eb, oout, inv_l):
    n = KC // BLK
    two = pl.ds(2 * i, 2)
    q = qr[two].reshape(QB, HD)
    total = jnp.zeros((8, QB), F32)
    acc = jnp.zeros((HD, QB), F32)
    for c in range(16 // n):
        keys = kr[c * n : (c + 1) * n].reshape(KC, HD)
        s = lax.dot_general(keys, q, NT, preferred_element_type=F32)
        e = jnp.exp2(s * LOG2E_SCALE)
        total = total + fold8(e)
        e16 = e.astype(BF16)
        eb[i, pl.ds(c * KC, KC), :] = e16
        acc = acc + jnp.dot(cat_t(vt, c, n), e16, preferred_element_type=F32)
    inv = 1.0 / jnp.sum(total, axis=0, keepdims=True)
    inv_l[i] = jnp.broadcast_to(inv, (8, QB))
    oout[two] = (acc * inv).T.astype(BF16).reshape(2, BLK, HD)


def backward(i, first, gin, vin, kr, krt, qr, oout, eb, inv_l, dkacc, dvacc, dqrot):
    n = KC // BLK
    two = pl.ds(2 * i, 2)
    g = gin[two].reshape(QB, HD).astype(F32)
    o = oout[two].reshape(QB, HD).astype(F32)
    inv = inv_l[i][0:1, :]
    delta = jnp.sum((g * o).T, axis=0, keepdims=True) * inv
    gt = (g.T * inv).astype(BF16)
    gs = gt.T
    q = qr[two].reshape(QB, HD)
    acc = jnp.zeros((HD, QB), F32)
    for c in range(16 // n):
        rows = pl.ds(c * KC, KC)
        e16 = eb[i, rows, :]
        values = vin[c * n : (c + 1) * n].reshape(KC, HD)
        dp = jnp.dot(values, gt, preferred_element_type=F32)
        ds = (e16.astype(F32) * (dp - delta)).astype(BF16)
        dv = jnp.dot(e16, gs, preferred_element_type=F32)
        dk = jnp.dot(ds, q, preferred_element_type=F32)
        if first:
            dvacc[rows, :] = dv
            dkacc[rows, :] = dk
        else:
            dvacc[rows, :] += dv
            dkacc[rows, :] += dk
        acc = acc + jnp.dot(cat_t(krt, c, n), ds, preferred_element_type=F32)
    dqrot[...] = (acc * SCALE).T.reshape(2, BLK, HD)


def finish(b, raw, d_rot, which, gains, cos_ref, sin_ref, out, gsum):
    d, txt, img = back_block(raw[b], d_rot, gain_rows(gains, which), cos_ref[...], sin_ref[...])
    out[b] = d
    gsum[which] += fold8(img)
    gsum[which + 2] += fold8(txt)


def spread(n, axis, fn):
    me = lax.axis_index(axis)

    def one(r, c):
        fn(lax.rem(me + r, n))
        return c

    lax.fori_loop(1, n, one, 0)


def barrier(axes):
    sem = pltpu.get_barrier_semaphore()
    for axis, n in axes:
        spread(n, axis, lambda d, axis=axis: pl.semaphore_signal(
            sem, inc=1, device_id={axis: d}, device_id_type=pl.DeviceIdType.MESH))
    pl.semaphore_wait(sem, sum(n - 1 for _, n in axes))


def remote(src, dst, send, recv, axis, d):
    return pltpu.make_async_remote_copy(src, dst, send, recv, device_id={axis: d}, device_id_type=pl.DeviceIdType.MESH)


def wait_bytes(ref, sem):
    pltpu.make_async_copy(ref, ref, sem).wait()


def head_columns(d):
    return pl.ds(pl.multiple_of(d * HD, HD), HD)


def joint_kernel(img, txt, img_cot, txt_cot, gains, rc, rs, cc, cs,
                 img_out, txt_out, img_grad, txt_grad, gain,
                 qin, kin, vin, gin, oout, dq, dk, dv,
                 cos_ref, sin_ref, kr, krt, vt, qr, eb, inv_l, dkacc, dvacc, dqrot, gsum,
                 part, rows, srow, srows, send, recv, osend, orecv, olocal, gsend, grecv):
    me, dp = lax.axis_index("seq"), lax.axis_index("dp")
    barrier((("seq", 16), ("dp", 32)))
    text, image = pl.ds(0, TXT_B), pl.ds(TXT_B, BLK - TXT_B)

    def pieces(slot, d):
        col = head_columns(d)
        if slot < 3:
            return txt.at[slot, :, col], img.at[slot, :, col]
        return txt_cot.at[:, col], img_cot.at[:, col]

    for slot, ref in ((1, kin), (2, vin), (0, qin), (3, gin)):
        def push(r, c, slot=slot, ref=ref):
            d = lax.rem(me + r, 16)
            t, i = pieces(slot, d)
            remote(t, ref.at[r, text], send.at[slot], recv.at[slot, r], "seq", d).start()
            remote(i, ref.at[r, image], send.at[slot], recv.at[slot, r], "seq", d).start()
            return c

        t, i = pieces(slot, me)
        pltpu.make_async_copy(t, ref.at[0, text], recv.at[slot, 0]).start()
        pltpu.make_async_copy(i, ref.at[0, image], recv.at[slot, 0]).start()
        lax.fori_loop(1, 16, push, 0)

    def source(r):
        return lax.rem(me + 16 - r, 16)

    col = head_columns(me)

    def targets(slot):
        if slot < 3:
            return txt_grad.at[slot, :, col], img_grad.at[slot, :, col]
        return txt_out.at[:, col], img_out.at[:, col]

    def push_back(slot, ref, r):
        t, i = targets(slot)

        @pl.when(r == 0)
        def _():
            pltpu.make_async_copy(ref.at[0, text], t, olocal.at[slot]).start()
            pltpu.make_async_copy(ref.at[0, image], i, olocal.at[slot]).start()

        @pl.when(r > 0)
        def _():
            d = source(r)
            remote(ref.at[r, text], t, osend.at[slot], orecv.at[slot], "seq", d).start()
            remote(ref.at[r, image], i, osend.at[slot], orecv.at[slot], "seq", d).start()

    fill_tables(rc, rs, cc, cs, cos_ref, sin_ref)
    gsum[...] = jnp.zeros_like(gsum)
    dkacc[...] = jnp.zeros_like(dkacc)
    dvacc[...] = jnp.zeros_like(dvacc)
    g = gains[...]

    def take_k(r, c):
        wait_bytes(kin.at[r], recv.at[1, r])
        s = source(r)
        k = rope_block(kin[r], gain_rows(g, 1), cos_ref[s], sin_ref[s])
        kr[r] = k
        krt[r] = k.T
        return c

    lax.fori_loop(0, 16, take_k, 0)

    def take_v(r, c):
        wait_bytes(vin.at[r], recv.at[2, r])
        vt[r] = vin[r].T
        return c

    lax.fori_loop(0, 16, take_v, 0)

    def ahead(i, c):
        for j in range(2):
            r = 2 * i + j
            wait_bytes(qin.at[r], recv.at[0, r])
            s = source(r)
            qr[r] = rope_block(qin[r], gain_rows(g, 0), cos_ref[s], sin_ref[s])
        forward(i, kr, vt, qr, eb, oout, inv_l)

        @pl.when(i > 0)
        def _():
            push_back(3, oout, 2 * i - 2)
            push_back(3, oout, 2 * i - 1)

        return c

    lax.fori_loop(0, 8, ahead, 0)

    def back(i, c):
        for j in range(2):
            wait_bytes(gin.at[2 * i + j], recv.at[3, 2 * i + j])

        @pl.when(i == 0)
        def _():
            push_back(3, oout, 14)
            push_back(3, oout, 15)

        backward(i, False, gin, vin, kr, krt, qr, oout, eb, inv_l, dkacc, dvacc, dqrot)
        for j in range(2):
            r = 2 * i + j
            s = source(r)
            finish(r, qin, dqrot[j], 0, g, cos_ref.at[s], sin_ref.at[s], dq, gsum)

        @pl.when(i > 0)
        def _():
            push_back(0, dq, 2 * i - 2)
            push_back(0, dq, 2 * i - 1)

        return c

    lax.fori_loop(0, 8, back, 0)

    def last_v(r, c):
        dv[r] = dvacc[pl.ds(pl.multiple_of(r * BLK, BLK), BLK), :].astype(BF16)
        return c

    lax.fori_loop(0, 16, last_v, 0)
    push_back(0, dq, 14)
    push_back(0, dq, 15)

    def last_k(r, c):
        s = source(r)
        push_back(2, dv, r)
        finish(r, kin, dkacc[pl.ds(pl.multiple_of(r * BLK, BLK), BLK), :] * SCALE, 1, g, cos_ref.at[s], sin_ref.at[s], dk, gsum)
        return c

    lax.fori_loop(0, 16, last_k, 0)
    for j in range(4):
        part[j] = jnp.sum(gsum[j], axis=0, keepdims=True)

    def send_k(r, c):
        push_back(1, dk, r)
        return c

    rows[dp] = part[dp // 8]
    lax.fori_loop(0, 8, send_k, 0)
    spread(32, "dp", lambda d: remote(part.at[d // 8], rows.at[dp], gsend.at[0], grecv.at[0], "dp", d).start())
    lax.fori_loop(8, 16, send_k, 0)
    wait_bytes(rows.at[pl.ds(0, 31)], grecv.at[0])
    srow[...] = jnp.sum(rows[...], axis=0)
    srows[me] = srow[...]
    for slot, ref in ((0, qin), (1, kin), (2, vin), (3, gin)):
        wait_bytes(ref.at[pl.ds(0, 15)], send.at[slot])
    spread(16, "seq", lambda d: remote(srow, srows.at[me], gsend.at[1], grecv.at[1], "seq", d).start())
    wait_bytes(srows.at[pl.ds(0, 15)], grecv.at[1])
    total = jnp.sum(srows[...], axis=0) * GRAD_SCALE
    gain[...] = pltpu.roll(jnp.broadcast_to(total, (8, HD)), lax.rem(HD - lax.rem(dp, 8) * 16, HD), axis=1)
    wait_bytes(rows.at[pl.ds(0, 31)], gsend.at[0])
    wait_bytes(srows.at[pl.ds(0, 15)], gsend.at[1])
    for slot, ref in ((0, dq), (1, dk), (2, dv), (3, oout)):
        wait_bytes(ref.at[0], olocal.at[slot])
        wait_bytes(ref.at[pl.ds(0, 15)], osend.at[slot])
        wait_bytes(ref.at[pl.ds(0, 15)], orecv.at[slot])


def compute_scratch():
    return [
        pltpu.VMEM((16, BLK, HD), F32), pltpu.VMEM((16, BLK, HD), F32),
        pltpu.VMEM((16, BLK, HD), BF16), pltpu.VMEM((16, HD, BLK), BF16), pltpu.VMEM((16, HD, BLK), BF16),
        pltpu.VMEM((16, BLK, HD), BF16),
        pltpu.VMEM((8, 2048, QB), BF16), pltpu.VMEM((8, 8, QB), F32),
        pltpu.VMEM((2048, HD), F32), pltpu.VMEM((2048, HD), F32),
        pltpu.VMEM((2, BLK, HD), F32), pltpu.VMEM((4, 8, HD), F32),
    ]


def per_device(img_qkv, txt_qkv, img_cot, txt_cot, norm_gains):
    img = jnp.transpose(img_qkv[0], (1, 0, 2))
    txt = jnp.transpose(txt_qkv[0], (1, 0, 2))
    any_, vmem = pl.BlockSpec(memory_space=pl.ANY), pl.BlockSpec(memory_space=pltpu.VMEM)
    dma = pltpu.SemaphoreType.DMA
    shape = lambda s: jax.ShapeDtypeStruct(s, BF16)
    n_img, n_txt, width = img.shape[1], txt.shape[1], img.shape[2]
    img_out, txt_out, img_grad, txt_grad, gain = pl.pallas_call(
        joint_kernel,
        out_shape=[shape((n_img, width)), shape((n_txt, width)), shape((3, n_img, width)), shape((3, n_txt, width)),
                   jax.ShapeDtypeStruct((8, HD), F32)],
        in_specs=[any_] * 4 + [vmem] * 5, out_specs=[any_] * 4 + [vmem],
        scratch_shapes=[pltpu.VMEM((16, BLK, HD), BF16)] * 8 + compute_scratch() + [
            pltpu.VMEM((4, 1, HD), F32), pltpu.VMEM((32, 1, HD), F32), pltpu.VMEM((1, HD), F32), pltpu.VMEM((16, 1, HD), F32),
            dma((4,)), dma((4, 16)), dma((4,)), dma((4,)), dma((4,)), dma((2,)), dma((2,))],
        compiler_params=pltpu.CompilerParams(collective_id=0, has_side_effects=True, vmem_limit_bytes=56 << 20),
    )(img, txt, img_cot[0], txt_cot[0], norm_gains, *[jnp.asarray(t) for t in small_tables(28)])
    return (img_out[None], txt_out[None], jnp.transpose(img_grad, (1, 0, 2))[None],
            jnp.transpose(txt_grad, (1, 0, 2))[None], gain[0, :16])


def solution(mesh):
    in_specs = (P("dp", "seq", None, None), P("dp", "seq", None, None), P("dp", "seq", None), P("dp", "seq", None), P())
    out_specs = (P("dp", "seq", None), P("dp", "seq", None), P("dp", "seq", None, None), P("dp", "seq", None, None), P("dp"))
    return jax.shard_map(per_device, mesh=mesh, in_specs=in_specs, out_specs=out_specs, check_vma=False)
```

```python
import functools
import math

import jax
import jax.numpy as jnp
import numpy as np
from jax import lax
from jax.experimental import pallas as pl
from jax.experimental.pallas import tpu as pltpu
from jax.sharding import PartitionSpec as P

HD = 128
GRID_W = 64
EPSILON = 1e-06
F32 = jnp.float32
BF16 = jnp.bfloat16
SCALE = 1.0 / math.sqrt(HD)
LOG2E_SCALE = SCALE * math.log2(math.e)
NT = (((1,), (1,)), ((), ()))
BLK = 128
DP_STAGES = ((2, 4, 6), (1, 16, 17), (8,))
TXT_B = 16
QB = 256
GRAD_SCALE = 1.0 / math.sqrt(32 * 2048 * 16)
KC = 512


def small_tables(n_rows):
    time_dims = HD // 8
    axis = (HD - time_dims) // 2
    channel = np.arange(HD)
    in_rows = (channel >= time_dims) & (channel < time_dims + axis)
    in_cols = channel >= time_dims + axis
    within = np.where(in_cols, channel - time_dims - axis, channel - time_dims)
    within = np.maximum(within, 0) // 2
    freq = np.power(10000.0, -2.0 * within / axis).astype(np.float32)
    sign = np.where(channel % 2 == 0, -1.0, 1.0)
    rows = np.arange(n_rows, dtype=np.float32)[:, None] * np.where(in_rows, freq, 0)[None, :]
    cols = np.arange(GRID_W, dtype=np.float32)[:, None] * np.where(in_cols, freq, 0)[None, :]
    rows, cols = rows.astype(np.float32).astype(np.float64), cols.astype(np.float32).astype(np.float64)
    out = [np.cos(rows), np.sin(rows) * sign, np.cos(cols), np.sin(cols) * sign]
    return [o.astype(np.float32) for o in out]


def fill_tables(rc, rs, cc, cs, cos_ref, sin_ref):
    lane = lax.broadcasted_iota(jnp.int32, (16, HD), 1)
    is_col = lane >= HD // 8 + (HD - HD // 8) // 2

    def text(b, c):
        cos_ref[b, pl.ds(0, TXT_B), :] = jnp.ones((TXT_B, HD), F32)
        sin_ref[b, pl.ds(0, TXT_B), :] = jnp.zeros((TXT_B, HD), F32)
        return c

    lax.fori_loop(0, 16, text, 0)

    def image(m, c):
        b, off = m // 7, pl.multiple_of(16 + 16 * (m % 7), 16)
        r, col = m // 4, pl.multiple_of(16 * (m % 4), 16)
        cos_ref[b, pl.ds(off, 16), :] = jnp.where(is_col, cc[pl.ds(col, 16), :], rc[pl.ds(r, 1), :])
        sin_ref[b, pl.ds(off, 16), :] = jnp.where(is_col, cs[pl.ds(col, 16), :], rs[pl.ds(r, 1), :])
        return c

    lax.fori_loop(0, 112, image, 0)


def swap_pairs(x):
    lane = lax.broadcasted_iota(jnp.int32, x.shape, x.ndim - 1)
    return jnp.where(lane % 2 == 0, pltpu.roll(x, HD - 1, axis=1), pltpu.roll(x, 1, axis=1))


def normed(x):
    inv = lax.rsqrt(jnp.mean(x * x, axis=-1, keepdims=True) + EPSILON)
    return x * inv, inv


def gain_rows(gains, which):
    row = lax.broadcasted_iota(jnp.int32, (BLK, HD), 0)
    img = jnp.broadcast_to(gains[which : which + 1, :], (BLK, HD))
    txt = jnp.broadcast_to(gains[which + 2 : which + 3, :], (BLK, HD))
    return jnp.where(row < TXT_B, txt, img)


def rope_block(raw, gain, cos, sin):
    hat, _ = normed(raw.astype(F32))
    x = hat * gain
    return (x * cos + swap_pairs(x) * sin).astype(BF16)


def back_block(raw, d_rot, gain, cos, sin):
    hat, inv = normed(raw.astype(F32))
    d_norm = d_rot * cos + swap_pairs(d_rot * sin)
    terms = d_norm * hat
    scaled = d_norm * gain
    middle = jnp.mean(scaled * hat, axis=-1, keepdims=True)
    return ((scaled - hat * middle) * inv).astype(BF16), terms[:TXT_B], terms[TXT_B:]


def fold8(x):
    total = x[0:8]
    for i in range(8, x.shape[0], 8):
        total = total + x[i : i + 8]
    return total


def cat_t(ref, c, n):
    return jnp.concatenate([ref[c * n + i] for i in range(n)], axis=1)


def forward(i, kr, vt, qr, eb, oout, inv_l):
    n = KC // BLK
    two = pl.ds(2 * i, 2)
    q = qr[two].reshape(QB, HD)
    total = jnp.zeros((8, QB), F32)
    acc = jnp.zeros((HD, QB), F32)
    for c in range(16 // n):
        keys = kr[c * n : (c + 1) * n].reshape(KC, HD)
        s = lax.dot_general(keys, q, NT, preferred_element_type=F32)
        e = jnp.exp2(s * LOG2E_SCALE)
        total = total + fold8(e)
        e16 = e.astype(BF16)
        eb[i, pl.ds(c * KC, KC), :] = e16
        acc = acc + jnp.dot(cat_t(vt, c, n), e16, preferred_element_type=F32)
    inv = 1.0 / jnp.sum(total, axis=0, keepdims=True)
    inv_l[i] = jnp.broadcast_to(inv, (8, QB))
    oout[two] = (acc * inv).T.astype(BF16).reshape(2, BLK, HD)


def backward(i, first, gin, vin, kr, krt, qr, oout, eb, inv_l, dkacc, dvacc, dqrot):
    n = KC // BLK
    two = pl.ds(2 * i, 2)
    g = gin[two].reshape(QB, HD).astype(F32)
    o = oout[two].reshape(QB, HD).astype(F32)
    inv = inv_l[i][0:1, :]
    delta = jnp.sum((g * o).T, axis=0, keepdims=True) * inv
    gt = (g.T * inv).astype(BF16)
    gs = gt.T
    q = qr[two].reshape(QB, HD)
    acc = jnp.zeros((HD, QB), F32)
    for c in range(16 // n):
        rows = pl.ds(c * KC, KC)
        e16 = eb[i, rows, :]
        values = vin[c * n : (c + 1) * n].reshape(KC, HD)
        dp = jnp.dot(values, gt, preferred_element_type=F32)
        ds = (e16.astype(F32) * (dp - delta)).astype(BF16)
        dv = jnp.dot(e16, gs, preferred_element_type=F32)
        dk = jnp.dot(ds, q, preferred_element_type=F32)
        if first:
            dvacc[rows, :] = dv
            dkacc[rows, :] = dk
        else:
            dvacc[rows, :] += dv
            dkacc[rows, :] += dk
        acc = acc + jnp.dot(cat_t(krt, c, n), ds, preferred_element_type=F32)
    dqrot[...] = (acc * SCALE).T.reshape(2, BLK, HD)


def finish(b, raw, d_rot, which, gains, cos_ref, sin_ref, out, gsum):
    d, txt, img = back_block(raw[b], d_rot, gain_rows(gains, which), cos_ref[...], sin_ref[...])
    out[b] = d
    gsum[which] += fold8(img)
    gsum[which + 2] += fold8(txt)


def flip(i, bits):
    for b in (1, 2, 4, 8, 16):
        if bits & b:
            i = i + b - 2 * b * (i // b % 2)
    return i


def spread(n, axis, fn):
    me = lax.axis_index(axis)

    def one(r, c):
        fn(lax.rem(me + r, n))
        return c

    lax.fori_loop(1, n, one, 0)


def barrier():
    sem = pltpu.get_barrier_semaphore()

    def greet(axis, d):
        pl.semaphore_signal(sem, inc=1, device_id={axis: d}, device_id_type=pl.DeviceIdType.MESH)

    spread(16, "seq", lambda d: greet("seq", d))
    dp = lax.axis_index("dp")
    for stage in DP_STAGES:
        for bits in stage:
            greet("dp", flip(dp, bits))
    pl.semaphore_wait(sem, 15 + sum(len(stage) for stage in DP_STAGES))


def remote(src, dst, send, recv, axis, d):
    return pltpu.make_async_remote_copy(src, dst, send, recv, device_id={axis: d}, device_id_type=pl.DeviceIdType.MESH)


def wait_bytes(ref, sem):
    pltpu.make_async_copy(ref, ref, sem).wait()


def head_columns(d):
    return pl.ds(pl.multiple_of(d * HD, HD), HD)


def joint_kernel(img, txt, img_cot, txt_cot, gains, rc, rs, cc, cs, back_out, gain,
                 qin, kin, vin, gin, oout, dq, dk, dv,
                 cos_ref, sin_ref, kr, krt, vt, qr, eb, inv_l, dkacc, dvacc, dqrot, gsum,
                 part, rows, srow, srows, send, recv, osend, orecv, olocal, gsend, grecv):
    me, dp = lax.axis_index("seq"), lax.axis_index("dp")
    barrier()
    text, image = pl.ds(0, TXT_B), pl.ds(TXT_B, BLK - TXT_B)

    def pieces(slot, d):
        col = head_columns(d)
        if slot < 3:
            return txt.at[slot, :, col], img.at[slot, :, col]
        return txt_cot.at[:, col], img_cot.at[:, col]

    for slot, ref in ((1, kin), (2, vin), (0, qin), (3, gin)):
        def push(r, c, slot=slot, ref=ref):
            d = lax.rem(me + r, 16)
            t, i = pieces(slot, d)
            remote(t, ref.at[r, text], send.at[slot], recv.at[slot, r], "seq", d).start()
            remote(i, ref.at[r, image], send.at[slot], recv.at[slot, r], "seq", d).start()
            return c

        t, i = pieces(slot, me)
        pltpu.make_async_copy(t, ref.at[0, text], recv.at[slot, 0]).start()
        pltpu.make_async_copy(i, ref.at[0, image], recv.at[slot, 0]).start()
        lax.fori_loop(1, 16, push, 0)

    def source(r):
        return lax.rem(me + 16 - r, 16)

    col = head_columns(me)

    def push_back(slot, ref, r):
        there = back_out.at[slot, :, col]

        @pl.when(r == 0)
        def _():
            pltpu.make_async_copy(ref.at[0], there, olocal.at[slot]).start()

        @pl.when(r > 0)
        def _():
            remote(ref.at[r], there, osend.at[slot], orecv.at[slot], "seq", source(r)).start()

    fill_tables(rc, rs, cc, cs, cos_ref, sin_ref)
    gsum[...] = jnp.zeros_like(gsum)
    dkacc[...] = jnp.zeros_like(dkacc)
    dvacc[...] = jnp.zeros_like(dvacc)
    g = gains[...]

    def take_k(r, c):
        wait_bytes(kin.at[r], recv.at[1, r])
        s = source(r)
        k = rope_block(kin[r], gain_rows(g, 1), cos_ref[s], sin_ref[s])
        kr[r] = k
        krt[r] = k.T
        return c

    lax.fori_loop(0, 16, take_k, 0)

    def take_v(r, c):
        wait_bytes(vin.at[r], recv.at[2, r])
        vt[r] = vin[r].T
        return c

    lax.fori_loop(0, 16, take_v, 0)

    def ahead(i, c):
        for j in range(2):
            r = 2 * i + j
            wait_bytes(qin.at[r], recv.at[0, r])
            s = source(r)
            qr[r] = rope_block(qin[r], gain_rows(g, 0), cos_ref[s], sin_ref[s])
        forward(i, kr, vt, qr, eb, oout, inv_l)

        @pl.when(i > 0)
        def _():
            push_back(3, oout, 2 * i - 2)
            push_back(3, oout, 2 * i - 1)

        return c

    lax.fori_loop(0, 8, ahead, 0)

    def back(i, c):
        for j in range(2):
            wait_bytes(gin.at[2 * i + j], recv.at[3, 2 * i + j])

        @pl.when(i == 0)
        def _():
            push_back(3, oout, 14)
            push_back(3, oout, 15)

        backward(i, False, gin, vin, kr, krt, qr, oout, eb, inv_l, dkacc, dvacc, dqrot)
        for j in range(2):
            r = 2 * i + j
            s = source(r)
            finish(r, qin, dqrot[j], 0, g, cos_ref.at[s], sin_ref.at[s], dq, gsum)

        @pl.when(i > 0)
        def _():
            push_back(0, dq, 2 * i - 2)
            push_back(0, dq, 2 * i - 1)

        return c

    lax.fori_loop(0, 8, back, 0)

    push_back(0, dq, 14)
    push_back(0, dq, 15)

    def last(r, c):
        s = source(r)
        rows_r = pl.ds(pl.multiple_of(r * BLK, BLK), BLK)
        dv[r] = dvacc[rows_r, :].astype(BF16)
        finish(r, kin, dkacc[rows_r, :] * SCALE, 1, g, cos_ref.at[s], sin_ref.at[s], dk, gsum)
        return c

    lax.fori_loop(0, 16, last, 0)
    for j in range(4):
        part[0, j : j + 1] = jnp.sum(gsum[j], axis=0, keepdims=True)

    def push_some(slot, ref, a, b):
        def one(r, c):
            push_back(slot, ref, r)
            return c

        lax.fori_loop(a, b, one, 0)

    bulk = ((2, dv, 0, 8), (2, dv, 8, 16), (1, dk, 0, 8), (1, dk, 8, 16))
    for n, stage in enumerate(DP_STAGES):
        for m, bits in enumerate(stage):
            remote(part.at[n], rows.at[n, m], gsend.at[n], grecv.at[n], "dp", flip(dp, bits)).start()
        push_some(*bulk[n])
        here = rows.at[n, pl.ds(0, len(stage))]
        wait_bytes(here, grecv.at[n])
        total = part[n]
        for m in range(len(stage)):
            total = total + rows[n, m]
        part[n + 1] = total
    srow[...] = part[3]
    spread(16, "seq", lambda d: remote(srow, srows.at[me], gsend.at[3], grecv.at[3], "seq", d).start())
    push_some(*bulk[3])
    srows[me] = srow[...]
    wait_bytes(srows.at[pl.ds(0, 15)], grecv.at[3])
    total = jnp.sum(srows[...], axis=0) * GRAD_SCALE
    line = jnp.zeros((1, HD), F32)
    for j in range(4):
        line = jnp.where(dp // 8 == j, total[j : j + 1], line)
    gain[...] = pltpu.roll(jnp.broadcast_to(line, (8, HD)), lax.rem(HD - lax.rem(dp, 8) * 16, HD), axis=1)
    for n, stage in enumerate(DP_STAGES):
        wait_bytes(rows.at[n, pl.ds(0, len(stage))], gsend.at[n])
    wait_bytes(srows.at[pl.ds(0, 15)], gsend.at[3])
    for slot, ref in ((0, qin), (1, kin), (2, vin), (3, gin)):
        wait_bytes(ref.at[pl.ds(0, 15)], send.at[slot])
    for slot, ref in ((3, oout), (0, dq), (2, dv), (1, dk)):
        wait_bytes(ref.at[0], olocal.at[slot])
        wait_bytes(ref.at[pl.ds(0, 15)], osend.at[slot])
        wait_bytes(ref.at[pl.ds(0, 15)], orecv.at[slot])


def emit_kernel(back_out, gain, img_out, txt_out, img_grad, txt_grad, gain_out, sems):
    text, image, grads = pl.ds(0, TXT_B), pl.ds(TXT_B, BLK - TXT_B), pl.ds(0, 3)
    copies = [
        pltpu.make_async_copy(back_out.at[grads, image], img_grad, sems.at[0]),
        pltpu.make_async_copy(back_out.at[3, image], img_out, sems.at[1]),
        pltpu.make_async_copy(back_out.at[grads, text], txt_grad, sems.at[2]),
        pltpu.make_async_copy(back_out.at[3, text], txt_out, sems.at[3]),
    ]
    for copy in copies:
        copy.start()
    gain_out[...] = gain[0:1, 0:16]
    for copy in copies:
        copy.wait()


def compute_scratch():
    return [
        pltpu.VMEM((16, BLK, HD), F32), pltpu.VMEM((16, BLK, HD), F32),
        pltpu.VMEM((16, BLK, HD), BF16), pltpu.VMEM((16, HD, BLK), BF16), pltpu.VMEM((16, HD, BLK), BF16),
        pltpu.VMEM((16, BLK, HD), BF16),
        pltpu.VMEM((8, 2048, QB), BF16), pltpu.VMEM((8, 8, QB), F32),
        pltpu.VMEM((2048, HD), F32), pltpu.VMEM((2048, HD), F32),
        pltpu.VMEM((2, BLK, HD), F32), pltpu.VMEM((4, 8, HD), F32),
    ]


def per_device(img_qkv, txt_qkv, img_cot, txt_cot, norm_gains):
    img = jnp.transpose(img_qkv[0], (1, 0, 2))
    txt = jnp.transpose(txt_qkv[0], (1, 0, 2))
    any_, vmem = pl.BlockSpec(memory_space=pl.ANY), pl.BlockSpec(memory_space=pltpu.VMEM)
    dma = pltpu.SemaphoreType.DMA
    shape = lambda s: jax.ShapeDtypeStruct(s, BF16)
    n_img, n_txt, width = img.shape[1], txt.shape[1], img.shape[2]
    back_out, gain = pl.pallas_call(
        joint_kernel,
        out_shape=[pltpu.VMEM((4, BLK, width), BF16), pltpu.VMEM((8, HD), F32)],
        in_specs=[any_] * 4 + [vmem] * 5, out_specs=[vmem] * 2,
        scratch_shapes=[pltpu.VMEM((16, BLK, HD), BF16)] * 8 + compute_scratch() + [
            pltpu.VMEM((4, 4, HD), F32), pltpu.VMEM((3, 3, 4, HD), F32), pltpu.VMEM((4, HD), F32), pltpu.VMEM((16, 4, HD), F32),
            dma((4,)), dma((4, 16)), dma((4,)), dma((4,)), dma((4,)), dma((4,)), dma((4,))],
        compiler_params=pltpu.CompilerParams(collective_id=0, has_side_effects=True, vmem_limit_bytes=58 << 20),
    )(img, txt, img_cot[0], txt_cot[0], norm_gains, *[jnp.asarray(t) for t in small_tables(28)])
    img_out, txt_out, img_grad, txt_grad, gain_out = pl.pallas_call(
        emit_kernel,
        out_shape=[shape((n_img, width)), shape((n_txt, width)), shape((3, n_img, width)), shape((3, n_txt, width)),
                   jax.ShapeDtypeStruct((1, 16), F32)],
        in_specs=[vmem] * 2, out_specs=[any_] * 4 + [vmem], scratch_shapes=[dma((4,))],
        compiler_params=pltpu.CompilerParams(vmem_limit_bytes=8 << 20),
    )(back_out, gain)
    return (img_out[None], txt_out[None], jnp.transpose(img_grad, (1, 0, 2))[None],
            jnp.transpose(txt_grad, (1, 0, 2))[None], gain_out.reshape(16))


def solution(mesh):
    in_specs = (P("dp", "seq", None, None), P("dp", "seq", None, None), P("dp", "seq", None), P("dp", "seq", None), P())
    out_specs = (P("dp", "seq", None), P("dp", "seq", None), P("dp", "seq", None, None), P("dp", "seq", None, None), P("dp"))
    return jax.shard_map(per_device, mesh=mesh, in_specs=in_specs, out_specs=out_specs, check_vma=False)
```

```python
import functools
import math

import jax
import jax.numpy as jnp
import numpy as np
from jax import lax
from jax.experimental import pallas as pl
from jax.experimental.pallas import tpu as pltpu
from jax.sharding import PartitionSpec as P

HD = 128
GRID_W = 64
EPSILON = 1e-06
F32 = jnp.float32
BF16 = jnp.bfloat16
SCALE = 1.0 / math.sqrt(HD)
LOG2E_SCALE = SCALE * math.log2(math.e)
NT = (((1,), (1,)), ((), ()))
BLK = 128
DP_STAGES = ((2, 4, 6), (1, 16, 17), (8,))
TXT_B = 16
QB = 256
GRAD_SCALE = 1.0 / math.sqrt(32 * 2048 * 16)
KC = 512


def small_tables(n_rows):
    time_dims = HD // 8
    axis = (HD - time_dims) // 2
    channel = np.arange(HD)
    in_rows = (channel >= time_dims) & (channel < time_dims + axis)
    in_cols = channel >= time_dims + axis
    within = np.where(in_cols, channel - time_dims - axis, channel - time_dims)
    within = np.maximum(within, 0) // 2
    freq = np.power(10000.0, -2.0 * within / axis).astype(np.float32)
    sign = np.where(channel % 2 == 0, -1.0, 1.0)
    rows = np.arange(n_rows, dtype=np.float32)[:, None] * np.where(in_rows, freq, 0)[None, :]
    cols = np.arange(GRID_W, dtype=np.float32)[:, None] * np.where(in_cols, freq, 0)[None, :]
    rows, cols = rows.astype(np.float32).astype(np.float64), cols.astype(np.float32).astype(np.float64)
    out = [np.cos(rows), np.sin(rows) * sign, np.cos(cols), np.sin(cols) * sign]
    return [o.astype(np.float32) for o in out]


def fill_tables(rc, rs, cc, cs, cos_ref, sin_ref):
    lane = lax.broadcasted_iota(jnp.int32, (16, HD), 1)
    is_col = lane >= HD // 8 + (HD - HD // 8) // 2

    def text(b, c):
        cos_ref[b, pl.ds(0, TXT_B), :] = jnp.ones((TXT_B, HD), F32)
        sin_ref[b, pl.ds(0, TXT_B), :] = jnp.zeros((TXT_B, HD), F32)
        return c

    lax.fori_loop(0, 16, text, 0)

    def image(m, c):
        b, off = m // 7, pl.multiple_of(16 + 16 * (m % 7), 16)
        r, col = m // 4, pl.multiple_of(16 * (m % 4), 16)
        cos_ref[b, pl.ds(off, 16), :] = jnp.where(is_col, cc[pl.ds(col, 16), :], rc[pl.ds(r, 1), :])
        sin_ref[b, pl.ds(off, 16), :] = jnp.where(is_col, cs[pl.ds(col, 16), :], rs[pl.ds(r, 1), :])
        return c

    lax.fori_loop(0, 112, image, 0)


def swap_pairs(x):
    lane = lax.broadcasted_iota(jnp.int32, x.shape, x.ndim - 1)
    return jnp.where(lane % 2 == 0, pltpu.roll(x, HD - 1, axis=1), pltpu.roll(x, 1, axis=1))


def normed(x):
    inv = lax.rsqrt(jnp.mean(x * x, axis=-1, keepdims=True) + EPSILON)
    return x * inv, inv


def gain_rows(gains, which):
    row = lax.broadcasted_iota(jnp.int32, (BLK, HD), 0)
    img = jnp.broadcast_to(gains[which : which + 1, :], (BLK, HD))
    txt = jnp.broadcast_to(gains[which + 2 : which + 3, :], (BLK, HD))
    return jnp.where(row < TXT_B, txt, img)


def rope_block(raw, gain, cos, sin):
    hat, _ = normed(raw.astype(F32))
    x = hat * gain
    return (x * cos + swap_pairs(x) * sin).astype(BF16)


def back_block(raw, d_rot, gain, cos, sin):
    hat, inv = normed(raw.astype(F32))
    d_norm = d_rot * cos + swap_pairs(d_rot * sin)
    terms = d_norm * hat
    scaled = d_norm * gain
    middle = jnp.mean(scaled * hat, axis=-1, keepdims=True)
    return ((scaled - hat * middle) * inv).astype(BF16), terms[:TXT_B], terms[TXT_B:]


def fold8(x):
    total = x[0:8]
    for i in range(8, x.shape[0], 8):
        total = total + x[i : i + 8]
    return total


def cat_t(ref, c, n):
    return jnp.concatenate([ref[c * n + i] for i in range(n)], axis=1)


def forward(i, kr, vt, qr, eb, oout, inv_l):
    n = KC // BLK
    two = pl.ds(2 * i, 2)
    q = qr[two].reshape(QB, HD)
    total = jnp.zeros((8, QB), F32)
    acc = jnp.zeros((HD, QB), F32)
    for c in range(16 // n):
        keys = kr[c * n : (c + 1) * n].reshape(KC, HD)
        s = lax.dot_general(keys, q, NT, preferred_element_type=F32)
        e = jnp.exp2(s * LOG2E_SCALE)
        total = total + fold8(e)
        e16 = e.astype(BF16)
        eb[i, pl.ds(c * KC, KC), :] = e16
        acc = acc + jnp.dot(cat_t(vt, c, n), e16, preferred_element_type=F32)
    inv = 1.0 / jnp.sum(total, axis=0, keepdims=True)
    inv_l[i] = jnp.broadcast_to(inv, (8, QB))
    oout[two] = (acc * inv).T.astype(BF16).reshape(2, BLK, HD)


def backward(i, first, gin, vin, kr, krt, qr, oout, eb, inv_l, dkacc, dvacc, dqrot):
    n = KC // BLK
    two = pl.ds(2 * i, 2)
    g = gin[two].reshape(QB, HD).astype(F32)
    o = oout[two].reshape(QB, HD).astype(F32)
    inv = inv_l[i][0:1, :]
    delta = jnp.sum((g * o).T, axis=0, keepdims=True) * inv
    gt = (g.T * inv).astype(BF16)
    gs = gt.T
    q = qr[two].reshape(QB, HD)
    acc = jnp.zeros((HD, QB), F32)
    for c in range(16 // n):
        rows = pl.ds(c * KC, KC)
        e16 = eb[i, rows, :]
        values = vin[c * n : (c + 1) * n].reshape(KC, HD)
        dp = jnp.dot(values, gt, preferred_element_type=F32)
        ds = (e16.astype(F32) * (dp - delta)).astype(BF16)
        dv = jnp.dot(e16, gs, preferred_element_type=F32)
        dk = jnp.dot(ds, q, preferred_element_type=F32)
        if first:
            dvacc[rows, :] = dv
            dkacc[rows, :] = dk
        else:
            dvacc[rows, :] += dv
            dkacc[rows, :] += dk
        acc = acc + jnp.dot(cat_t(krt, c, n), ds, preferred_element_type=F32)
    dqrot[...] = (acc * SCALE).T.reshape(2, BLK, HD)


def finish(b, raw, d_rot, which, gains, cos_ref, sin_ref, out, gsum):
    d, txt, img = back_block(raw[b], d_rot, gain_rows(gains, which), cos_ref[...], sin_ref[...])
    out[b] = d
    gsum[which] += fold8(img)
    gsum[which + 2] += fold8(txt)


def flip(i, bits):
    for b in (1, 2, 4, 8, 16):
        if bits & b:
            i = i + b - 2 * b * (i // b % 2)
    return i


def spread(n, axis, fn):
    me = lax.axis_index(axis)

    def one(r, c):
        fn(lax.rem(me + r, n))
        return c

    lax.fori_loop(1, n, one, 0)


def barrier():
    sem = pltpu.get_barrier_semaphore()

    def greet(axis, d):
        pl.semaphore_signal(sem, inc=1, device_id={axis: d}, device_id_type=pl.DeviceIdType.MESH)

    spread(16, "seq", lambda d: greet("seq", d))
    dp = lax.axis_index("dp")
    for stage in DP_STAGES:
        for bits in stage:
            greet("dp", flip(dp, bits))
    pl.semaphore_wait(sem, 15 + sum(len(stage) for stage in DP_STAGES))


def remote(src, dst, send, recv, axis, d):
    return pltpu.make_async_remote_copy(src, dst, send, recv, device_id={axis: d}, device_id_type=pl.DeviceIdType.MESH)


def wait_bytes(ref, sem):
    pltpu.make_async_copy(ref, ref, sem).wait()


def head_columns(d):
    return pl.ds(pl.multiple_of(d * HD, HD), HD)


def joint_kernel(img, txt, img_cot, txt_cot, gains, rc, rs, cc, cs, back_out, gain,
                 qin, kin, vin, gin, oout, dq, dk, dv,
                 cos_ref, sin_ref, kr, krt, vt, qr, eb, inv_l, dkacc, dvacc, dqrot, gsum,
                 part, rows, srow, srows, send, recv, osend, orecv, olocal, gsend, grecv):
    me, dp = lax.axis_index("seq"), lax.axis_index("dp")
    barrier()
    text, image = pl.ds(0, TXT_B), pl.ds(TXT_B, BLK - TXT_B)

    def pieces(slot, d):
        col = head_columns(d)
        if slot < 3:
            return txt.at[slot, :, col], img.at[slot, :, col]
        return txt_cot.at[:, col], img_cot.at[:, col]

    for slot, ref in ((1, kin), (2, vin), (0, qin), (3, gin)):
        def push(r, c, slot=slot, ref=ref):
            d = lax.rem(me + r, 16)
            t, i = pieces(slot, d)
            remote(t, ref.at[r, text], send.at[slot], recv.at[slot, r], "seq", d).start()
            remote(i, ref.at[r, image], send.at[slot], recv.at[slot, r], "seq", d).start()
            return c

        t, i = pieces(slot, me)
        pltpu.make_async_copy(t, ref.at[0, text], recv.at[slot, 0]).start()
        pltpu.make_async_copy(i, ref.at[0, image], recv.at[slot, 0]).start()
        lax.fori_loop(1, 16, push, 0)

    def source(r):
        return lax.rem(me + 16 - r, 16)

    col = head_columns(me)

    def push_back(slot, ref, r):
        there = back_out.at[slot, :, col]

        @pl.when(r == 0)
        def _():
            pltpu.make_async_copy(ref.at[0], there, olocal.at[slot]).start()

        @pl.when(r > 0)
        def _():
            remote(ref.at[r], there, osend.at[slot], orecv.at[slot], "seq", source(r)).start()

    fill_tables(rc, rs, cc, cs, cos_ref, sin_ref)
    gsum[...] = jnp.zeros_like(gsum)
    dkacc[...] = jnp.zeros_like(dkacc)
    dvacc[...] = jnp.zeros_like(dvacc)
    g = gains[...]

    def take_k(r, c):
        wait_bytes(kin.at[r], recv.at[1, r])
        s = source(r)
        k = rope_block(kin[r], gain_rows(g, 1), cos_ref[s], sin_ref[s])
        kr[r] = k
        krt[r] = k.T
        return c

    lax.fori_loop(0, 16, take_k, 0)

    def take_v(r, c):
        wait_bytes(vin.at[r], recv.at[2, r])
        vt[r] = vin[r].T
        return c

    lax.fori_loop(0, 16, take_v, 0)

    def ahead(i, c):
        for j in range(2):
            r = 2 * i + j
            wait_bytes(qin.at[r], recv.at[0, r])
            s = source(r)
            qr[r] = rope_block(qin[r], gain_rows(g, 0), cos_ref[s], sin_ref[s])
        forward(i, kr, vt, qr, eb, oout, inv_l)

        @pl.when(i > 0)
        def _():
            push_back(3, oout, 2 * i - 2)
            push_back(3, oout, 2 * i - 1)

        return c

    lax.fori_loop(0, 8, ahead, 0)

    def back(i, c):
        for j in range(2):
            wait_bytes(gin.at[2 * i + j], recv.at[3, 2 * i + j])

        @pl.when(i == 0)
        def _():
            push_back(3, oout, 14)
            push_back(3, oout, 15)

        backward(i, False, gin, vin, kr, krt, qr, oout, eb, inv_l, dkacc, dvacc, dqrot)
        for j in range(2):
            r = 2 * i + j
            s = source(r)
            finish(r, qin, dqrot[j], 0, g, cos_ref.at[s], sin_ref.at[s], dq, gsum)

        @pl.when(i > 0)
        def _():
            push_back(0, dq, 2 * i - 2)
            push_back(0, dq, 2 * i - 1)

        return c

    lax.fori_loop(0, 8, back, 0)

    push_back(0, dq, 14)
    push_back(0, dq, 15)

    def last(r, c):
        s = source(r)
        rows_r = pl.ds(pl.multiple_of(r * BLK, BLK), BLK)
        dv[r] = dvacc[rows_r, :].astype(BF16)
        finish(r, kin, dkacc[rows_r, :] * SCALE, 1, g, cos_ref.at[s], sin_ref.at[s], dk, gsum)
        return c

    lax.fori_loop(0, 16, last, 0)
    for j in range(4):
        part[0, j : j + 1] = jnp.sum(gsum[j], axis=0, keepdims=True)

    def push_some(slot, ref, a, b):
        def one(r, c):
            push_back(slot, ref, lax.rem(16 - r, 16))
            return c

        lax.fori_loop(a, b, one, 0)

    bulk = ((2, dv, 0, 8), (2, dv, 8, 16), (1, dk, 0, 8), (1, dk, 8, 16))
    for n, stage in enumerate(DP_STAGES):
        for m, bits in enumerate(stage):
            remote(part.at[n], rows.at[n, m], gsend.at[n], grecv.at[n], "dp", flip(dp, bits)).start()
        push_some(*bulk[n])
        here = rows.at[n, pl.ds(0, len(stage))]
        wait_bytes(here, grecv.at[n])
        total = part[n]
        for m in range(len(stage)):
            total = total + rows[n, m]
        part[n + 1] = total
    srow[...] = part[3]
    spread(16, "seq", lambda d: remote(srow, srows.at[me], gsend.at[3], grecv.at[3], "seq", d).start())
    push_some(*bulk[3])
    srows[me] = srow[...]
    wait_bytes(srows.at[pl.ds(0, 15)], grecv.at[3])
    total = jnp.sum(srows[...], axis=0) * GRAD_SCALE
    line = jnp.zeros((1, HD), F32)
    for j in range(4):
        line = jnp.where(dp // 8 == j, total[j : j + 1], line)
    gain[...] = pltpu.roll(jnp.broadcast_to(line, (8, HD)), lax.rem(HD - lax.rem(dp, 8) * 16, HD), axis=1)
    for n, stage in enumerate(DP_STAGES):
        wait_bytes(rows.at[n, pl.ds(0, len(stage))], gsend.at[n])
    wait_bytes(srows.at[pl.ds(0, 15)], gsend.at[3])
    for slot, ref in ((0, qin), (1, kin), (2, vin), (3, gin)):
        wait_bytes(ref.at[pl.ds(0, 15)], send.at[slot])
    for slot, ref in ((3, oout), (0, dq), (2, dv), (1, dk)):
        wait_bytes(ref.at[0], olocal.at[slot])
        wait_bytes(ref.at[pl.ds(0, 15)], osend.at[slot])
        wait_bytes(ref.at[pl.ds(0, 15)], orecv.at[slot])


def emit_kernel(back_out, gain, img_out, txt_out, img_grad, txt_grad, gain_out, sems):
    text, image, grads = pl.ds(0, TXT_B), pl.ds(TXT_B, BLK - TXT_B), pl.ds(0, 3)
    copies = [
        pltpu.make_async_copy(back_out.at[grads, image], img_grad, sems.at[0]),
        pltpu.make_async_copy(back_out.at[3, image], img_out, sems.at[1]),
        pltpu.make_async_copy(back_out.at[grads, text], txt_grad, sems.at[2]),
        pltpu.make_async_copy(back_out.at[3, text], txt_out, sems.at[3]),
    ]
    for copy in copies:
        copy.start()
    gain_out[...] = gain[0:1, 0:16]
    for copy in copies:
        copy.wait()


def compute_scratch():
    return [
        pltpu.VMEM((16, BLK, HD), F32), pltpu.VMEM((16, BLK, HD), F32),
        pltpu.VMEM((16, BLK, HD), BF16), pltpu.VMEM((16, HD, BLK), BF16), pltpu.VMEM((16, HD, BLK), BF16),
        pltpu.VMEM((16, BLK, HD), BF16),
        pltpu.VMEM((8, 2048, QB), BF16), pltpu.VMEM((8, 8, QB), F32),
        pltpu.VMEM((2048, HD), F32), pltpu.VMEM((2048, HD), F32),
        pltpu.VMEM((2, BLK, HD), F32), pltpu.VMEM((4, 8, HD), F32),
    ]


def per_device(img_qkv, txt_qkv, img_cot, txt_cot, norm_gains):
    img = jnp.transpose(img_qkv[0], (1, 0, 2))
    txt = jnp.transpose(txt_qkv[0], (1, 0, 2))
    any_, vmem = pl.BlockSpec(memory_space=pl.ANY), pl.BlockSpec(memory_space=pltpu.VMEM)
    dma = pltpu.SemaphoreType.DMA
    shape = lambda s: jax.ShapeDtypeStruct(s, BF16)
    n_img, n_txt, width = img.shape[1], txt.shape[1], img.shape[2]
    back_out, gain = pl.pallas_call(
        joint_kernel,
        out_shape=[pltpu.VMEM((4, BLK, width), BF16), pltpu.VMEM((8, HD), F32)],
        in_specs=[any_] * 4 + [vmem] * 5, out_specs=[vmem] * 2,
        scratch_shapes=[pltpu.VMEM((16, BLK, HD), BF16)] * 8 + compute_scratch() + [
            pltpu.VMEM((4, 4, HD), F32), pltpu.VMEM((3, 3, 4, HD), F32), pltpu.VMEM((4, HD), F32), pltpu.VMEM((16, 4, HD), F32),
            dma((4,)), dma((4, 16)), dma((4,)), dma((4,)), dma((4,)), dma((4,)), dma((4,))],
        compiler_params=pltpu.CompilerParams(collective_id=0, has_side_effects=True, vmem_limit_bytes=58 << 20),
    )(img, txt, img_cot[0], txt_cot[0], norm_gains, *[jnp.asarray(t) for t in small_tables(28)])
    img_out, txt_out, img_grad, txt_grad, gain_out = pl.pallas_call(
        emit_kernel,
        out_shape=[shape((n_img, width)), shape((n_txt, width)), shape((3, n_img, width)), shape((3, n_txt, width)),
                   jax.ShapeDtypeStruct((1, 16), F32)],
        in_specs=[vmem] * 2, out_specs=[any_] * 4 + [vmem], scratch_shapes=[dma((4,))],
        compiler_params=pltpu.CompilerParams(vmem_limit_bytes=8 << 20),
    )(back_out, gain)
    return (img_out[None], txt_out[None], jnp.transpose(img_grad, (1, 0, 2))[None],
            jnp.transpose(txt_grad, (1, 0, 2))[None], gain_out.reshape(16))


def solution(mesh):
    in_specs = (P("dp", "seq", None, None), P("dp", "seq", None, None), P("dp", "seq", None), P("dp", "seq", None), P())
    out_specs = (P("dp", "seq", None), P("dp", "seq", None), P("dp", "seq", None, None), P("dp", "seq", None, None), P("dp"))
    return jax.shard_map(per_device, mesh=mesh, in_specs=in_specs, out_specs=out_specs, check_vma=False)
```
